512 devices in a mesh: cell: 32 (over x, y, core), blk: 16 (over z).
Axes of the slice: x: 4, y: 4, z: 16, core: 2. Of those that a mesh axis runs over, the one named last changes fastest.
Arguments:
- snapshots: float32 [512, 65536], P('blk', 'cell'), may hold values from -100 to 100
- plan: int32 [31, 32], replicated, may hold values from 0 to 31, as said below
Outputs:
- energy_field: float32 [512, 65536], P('blk', 'cell')
- mode_energy: float32 [512], P('blk')
The draws below stay inside these ranges and needn't reach their ends.
Inputs may be any that keep to these rules, and one draw needn't show every extreme that they name: `plan`: each row pairs every index 0 .. 31 with exactly one other index (the partner's partner is the index itself, never the index), and over all rows every two indices are paired exactly once.
All inputs are finite; a program needn't handle non-finite values.
Results may differ from the reference program's by a relative error of at most 0.0055.
Values sent between devices are 32-bit elements; how exact they have to be, the bound alone decides.
A program may use at most 64 MiB of HBM per device.

```python
from functools import partial
import jax
import jax.numpy as jnp
from jax import lax

BW = 16
PAIRW = 32
COLS = 512
ROWS = 65536
ROUNDS = 7
N_BLK = 16


def draw_snapshots(key, part):
    key_column, key_row, key_noise = jax.random.split(jax.random.fold_in(key, 11), 3)
    column_scale = jnp.exp(jax.random.uniform(key_column, (COLS, 1), jnp.float32, jnp.log(0.3), jnp.log(3.0)))
    row_scale = jnp.exp(jax.random.uniform(key_row, (1, ROWS), jnp.float32, jnp.log(0.3), jnp.log(3.0)))
    values = jnp.clip(jax.random.normal(key_noise, (COLS, ROWS), jnp.float32), -5.0, 5.0)
    return (values * column_scale * row_scale).astype(jnp.float32)


def draw_plan(key, part):
    players = PAIRW - 1
    relabel = jax.random.permutation(jax.random.fold_in(key, 23), PAIRW).astype(jnp.int32)
    steps_col = jnp.arange(players, dtype=jnp.int32)[:, None]
    indices = jnp.arange(PAIRW, dtype=jnp.int32)[None, :]
    mirrored = jnp.mod(2 * steps_col - indices, players)
    circle_table = jnp.where(indices == players, steps_col, jnp.where(mirrored == indices, players, mirrored))
    circle_table = circle_table.astype(jnp.int32)
    mapped = relabel[circle_table]
    table = jnp.zeros((players, PAIRW), jnp.int32).at[:, relabel].set(mapped)
    return table


def setup_inputs(seed: int = 0) -> dict:
    seeds = jax.random.split(jax.random.key(seed), 3)
    snapshots = draw_snapshots(jax.random.fold_in(seeds[2], 71), 0)
    plan = draw_plan(jax.random.fold_in(seeds[2], 71), 0)
    return dict(snapshots=snapshots, plan=plan)


def inner_sweep(gram_whole, plan):
    pair_width = gram_whole.shape[0]
    positions = jnp.arange(pair_width, dtype=jnp.int32)

    def one_step(step_index, loop_state):
        gram_now, accumulated = loop_state
        partner = lax.dynamic_index_in_dim(plan, step_index, 0, keepdims=False)
        onehot = (partner[:, None] == positions[None, :]).astype(jnp.float32)
        symmetric = 0.5 * (gram_now + gram_now.T)
        own_diag = jnp.diagonal(symmetric)
        cross_term = jnp.sum(onehot * symmetric, axis=1)
        other_diag = jnp.sum(onehot * own_diag[None, :], axis=1)
        is_lower = positions < partner
        spread = jnp.where(is_lower, own_diag - other_diag, other_diag - own_diag)
        angles = 0.5 * jnp.arctan2(2.0 * cross_term, spread)
        cosine = jnp.cos(angles)
        sine_part = jnp.where(is_lower, jnp.sin(angles), -jnp.sin(angles))
        rotation_step = jnp.diag(cosine) + (onehot * sine_part[:, None]).T
        gram_now = jnp.dot(jnp.dot(rotation_step.T, gram_now, precision=lax.Precision.HIGHEST), rotation_step, precision=lax.Precision.HIGHEST)
        accumulated = jnp.dot(accumulated, rotation_step, precision=lax.Precision.HIGHEST)
        return gram_now, accumulated

    initial = (gram_whole, jnp.eye(pair_width, dtype=jnp.float32))
    return lax.fori_loop(0, pair_width - 1, one_step, initial)[1]


def pair_turn(stacked_pair, plan):
    gram_whole = jnp.dot(stacked_pair, stacked_pair.T, precision=lax.Precision.HIGHEST)
    turning = inner_sweep(gram_whole, plan)
    return jnp.dot(turning.T, stacked_pair, precision=lax.Precision.HIGHEST)


def reference(snapshots, plan):
    arranged = snapshots.reshape(N_BLK, 2, BW, ROWS)

    def one_round(loop_state, unused):
        upper_blocks, lower_blocks = loop_state
        stacked = jnp.concatenate([upper_blocks, lower_blocks], axis=1)
        turned = lax.map(partial(pair_turn, plan=plan), stacked)
        upper_new = turned[:, :BW]
        lower_new = turned[:, BW:]
        new_upper = jnp.concatenate([upper_new[:1], lower_new[:1], upper_new[1:-1]], axis=0)
        new_lower = jnp.concatenate([lower_new[1:], upper_new[-1:]], axis=0)
        return (new_upper, new_lower), None

    final_state, unused = lax.scan(one_round, (arranged[:, 0], arranged[:, 1]), None, length=ROUNDS)
    finished = jnp.concatenate([final_state[0], final_state[1]], axis=1).reshape(COLS, ROWS)
    energy_field = finished * finished
    mode_energy = jnp.sum(energy_field, axis=1) / ROWS
    return energy_field, mode_energy
```

```python
import functools

import jax
import jax.numpy as jnp
from jax import lax
from jax.experimental import pallas as pl
from jax.experimental.pallas import tpu as pltpu
from jax.sharding import PartitionSpec as P

ROUNDS = 7
INNER = 8
WIDTH = 32
HALF = 16
LANES = 128
MESH = pl.DeviceIdType.MESH
HIGHEST = lax.Precision.HIGHEST


def turn_of(own, other, cross, lower):
    difference = own - other
    spread = jnp.where(lower, difference, -difference)
    height = 2.0 * cross
    size = jnp.maximum(jnp.abs(height), jnp.abs(spread))
    nothing = size == 0.0
    factor = pl.reciprocal(jnp.where(nothing, 1.0, size), approx=True)
    y = height * factor
    d = jnp.where(nothing, 1.0, spread * factor)
    inverse = lax.rsqrt(y * y + d * d)
    half_up = 0.5 + 0.5 * jnp.abs(d) * inverse
    root = lax.rsqrt(half_up)
    large = half_up * root
    small = 0.5 * jnp.abs(y) * inverse * root
    ahead = d >= 0.0
    cosine = jnp.where(ahead, large, small)
    sine = jnp.where(ahead, small, large)
    sine = jnp.where(y < 0.0, -sine, sine)
    return cosine, jnp.where(lower, sine, -sine)


def permuted(value, index):
    return jnp.take_along_axis(value, index, axis=1, mode="promise_in_bounds")


def sweep(gram, plan_ref):
    shape = (WIDTH, LANES)
    row = lax.broadcasted_iota(jnp.int32, shape, 0)
    lane = lax.broadcasted_iota(jnp.int32, shape, 1)
    own_mask = row == lane
    lane_row = lax.broadcasted_iota(jnp.int32, (1, LANES), 1)

    def step(k, state):
        gram, turning = state
        partner = plan_ref[pl.ds(k, 1), :]
        index = jnp.broadcast_to(partner, shape)
        partner_mask = row == index
        crossed = permuted(gram, index)
        own = jnp.sum(jnp.where(own_mask, gram, 0.0), axis=0, keepdims=True)
        cross = jnp.sum(jnp.where(own_mask, crossed, 0.0), axis=0, keepdims=True)
        other = jnp.sum(jnp.where(partner_mask, crossed, 0.0), axis=0, keepdims=True)
        cosine, sine = turn_of(own, other, cross, lane_row < partner)
        half_done = gram * cosine + crossed * sine
        flipped = half_done.T[:WIDTH]
        flipped = jnp.concatenate([flipped, jnp.zeros((WIDTH, LANES - WIDTH), jnp.float32)], axis=1)
        gram = flipped * cosine + permuted(flipped, index) * sine
        turning = turning * cosine + permuted(turning, index) * sine
        return gram, turning

    start = jnp.where(own_mask, 1.0, 0.0).astype(jnp.float32)
    return lax.fori_loop(0, WIDTH - 1, step, (gram, start))[1]


def kernel(groups, blocks, snap_ref, plan_ref, out_ref, mode_ref,
           current, rotated, inner_slots, outer_slots,
           inner_send, inner_recv, outer_send, outer_recv, move_send, move_recv):
    cell = lax.axis_index("cell")
    pair = lax.axis_index("blk")
    inner = lax.rem(cell, INNER)
    outer = cell // INNER
    base = outer * INNER

    def inner_peer(offset):
        return lax.rem(inner + offset, INNER)

    def outer_peer(offset):
        return lax.rem(outer + offset, groups)

    barrier = pltpu.get_barrier_semaphore()
    for offset in range(1, INNER):
        pl.semaphore_signal(barrier, inc=1, device_id=(base + inner_peer(offset), pair), device_id_type=MESH)
    for offset in range(1, groups):
        pl.semaphore_signal(barrier, inc=1, device_id=(outer_peer(offset) * INNER + inner, pair), device_id_type=MESH)

    for step in (1, blocks - 1):
        pl.semaphore_signal(barrier, inc=1, device_id=(cell, lax.rem(pair + step, blocks)), device_id_type=MESH)
    pl.semaphore_wait(barrier, INNER - 1 + groups - 1 + 2)

    def inner_copy(slot, whose, peer, offset):
        return pltpu.make_async_remote_copy(
            src_ref=inner_slots.at[slot, whose], dst_ref=inner_slots.at[slot, whose],
            send_sem=inner_send.at[slot, offset], recv_sem=inner_recv.at[slot, whose],
            device_id=(base + peer, pair), device_id_type=MESH)

    def outer_copy(slot, whose, peer, offset):
        return pltpu.make_async_remote_copy(
            src_ref=outer_slots.at[slot, whose], dst_ref=outer_slots.at[slot, whose],
            send_sem=outer_send.at[slot, offset], recv_sem=outer_recv.at[slot, whose],
            device_id=(peer * INNER + inner, pair), device_id_type=MESH)

    def summed_gram(slot):
        block = current[slot].reshape(WIDTH, -1)
        gram = lax.dot_general(block, block, (((1,), (1,)), ((), ())), precision=HIGHEST,
                               preferred_element_type=jnp.float32)
        packed = jnp.concatenate([gram[8 * i:8 * i + 8] for i in range(4)], axis=1)
        inner_slots[slot, inner] = packed
        for offset in range(1, INNER):
            inner_copy(slot, inner, inner_peer(offset), offset).start()
        for offset in range(1, INNER):
            inner_copy(slot, inner_peer(offset), inner_peer(offset), offset).wait_recv()
        total = inner_slots[slot, 0]
        for i in range(1, INNER):
            total = total + inner_slots[slot, i]
        outer_slots[slot, outer] = total
        for offset in range(1, groups):
            outer_copy(slot, outer, outer_peer(offset), offset).start()
        for offset in range(1, groups):
            outer_copy(slot, outer_peer(offset), outer_peer(offset), offset).wait_recv()
        total = outer_slots[slot, 0]
        for i in range(1, groups):
            total = total + outer_slots[slot, i]
        for offset in range(1, INNER):
            inner_copy(slot, inner, inner_peer(offset), offset).wait_send()
        for offset in range(1, groups):
            outer_copy(slot, outer, outer_peer(offset), offset).wait_send()
        return jnp.concatenate(
            [total] + [pltpu.roll(total, LANES - WIDTH * i, 1) for i in range(1, 4)], axis=0)

    def right_copy(after):
        return pltpu.make_async_remote_copy(
            src_ref=rotated.at[jnp.where(pair == 0, 1, 0)], dst_ref=current.at[after, 0],
            send_sem=move_send.at[0], recv_sem=move_recv.at[after, 0],
            device_id=(cell, jnp.minimum(pair + 1, blocks - 1)), device_id_type=MESH)

    def left_copy(after):
        return pltpu.make_async_remote_copy(
            src_ref=rotated.at[1], dst_ref=current.at[after, 1],
            send_sem=move_send.at[1], recv_sem=move_recv.at[after, 1],
            device_id=(cell, jnp.maximum(pair - 1, 0)), device_id_type=MESH)

    current[0] = snap_ref[...].reshape(2, HALF, -1)

    def one_round(r, carry):
        now = lax.rem(r, 2)
        after = 1 - now
        turning = sweep(summed_gram(now), plan_ref)
        block = current[now].reshape(WIDTH, -1)
        turned = lax.dot_general(turning[:, :WIDTH], block, (((0,), (0,)), ((), ())), precision=HIGHEST,
                                 preferred_element_type=jnp.float32)
        rotated[...] = turned.reshape(2, HALF, -1)

        @pl.when(pair < blocks - 1)
        def _():
            right_copy(after).start()

        @pl.when(pair > 0)
        def _():
            left_copy(after).start()

        @pl.when(pair == 0)
        def _():
            current[after, 0] = rotated[0]

        @pl.when(pair == blocks - 1)
        def _():
            current[after, 1] = rotated[0]

        @pl.when(pair > 0)
        def _():
            right_copy(after).wait_recv()
            left_copy(after).wait_send()

        @pl.when(pair < blocks - 1)
        def _():
            left_copy(after).wait_recv()
            right_copy(after).wait_send()

        return carry

    lax.fori_loop(0, ROUNDS, one_round, 0)
    last = ROUNDS % 2
    gram = summed_gram(last)
    row = lax.broadcasted_iota(jnp.int32, (WIDTH, LANES), 0)
    lane = lax.broadcasted_iota(jnp.int32, (WIDTH, LANES), 1)
    mode_ref[...] = jnp.sum(jnp.where(row == lane, gram, 0.0), axis=0, keepdims=True)
    out_ref[...] = current[last].reshape(WIDTH, -1)


def on_device(snapshots, plan):
    cells = lax.axis_size("cell")
    blocks = lax.axis_size("blk")
    groups = cells // INNER
    local = snapshots.shape[1]
    steps = plan.shape[0]
    rest = jnp.broadcast_to(jnp.arange(WIDTH, LANES, dtype=jnp.int32), (steps, LANES - WIDTH))
    partners = jnp.concatenate([plan, rest], axis=1)
    field, energy = pl.pallas_call(
        functools.partial(kernel, groups, blocks),
        out_shape=(jax.ShapeDtypeStruct((WIDTH, local), jnp.float32),
                   jax.ShapeDtypeStruct((1, LANES), jnp.float32)),
        in_specs=[pl.BlockSpec(memory_space=pltpu.VMEM)] * 2,
        out_specs=(pl.BlockSpec(memory_space=pltpu.VMEM),) * 2,
        scratch_shapes=[
            pltpu.VMEM((2, 2, HALF, local), jnp.float32),
            pltpu.VMEM((2, HALF, local), jnp.float32),
            pltpu.VMEM((2, INNER, 8, LANES), jnp.float32),
            pltpu.VMEM((2, groups, 8, LANES), jnp.float32),
            pltpu.SemaphoreType.DMA((2, INNER)),
            pltpu.SemaphoreType.DMA((2, INNER)),
            pltpu.SemaphoreType.DMA((2, groups)),
            pltpu.SemaphoreType.DMA((2, groups)),
            pltpu.SemaphoreType.DMA((2,)),
            pltpu.SemaphoreType.DMA((2, 2)),
        ],
        compiler_params=pltpu.CompilerParams(collective_id=0, has_side_effects=True),
        name="rounds",
    )(snapshots, partners)
    return field * field, energy[0, :WIDTH] / (local * cells)


def solution(mesh):
    return jax.shard_map(
        on_device,
        mesh=mesh,
        in_specs=(P("blk", "cell"), P()),
        out_specs=(P("blk", "cell"), P("blk")),
        check_vma=False,
    )
```

```python
import functools

import jax
import jax.numpy as jnp
from jax import lax
from jax.experimental import pallas as pl
from jax.experimental.pallas import tpu as pltpu
from jax.sharding import PartitionSpec as P

ROUNDS = 7
INNER = 8
WIDTH = 32
HALF = 16
LANES = 128
CHUNKS = 4
MESH = pl.DeviceIdType.MESH
HIGHEST = lax.Precision.HIGHEST


def turn_of(own, other, cross, lower):
    difference = own - other
    spread = jnp.where(lower, difference, -difference)
    height = 2.0 * cross
    size = jnp.maximum(jnp.abs(height), jnp.abs(spread))
    nothing = size == 0.0
    factor = pl.reciprocal(jnp.where(nothing, 1.0, size), approx=True)
    y = height * factor
    d = jnp.where(nothing, 1.0, spread * factor)
    square = y * y + d * d
    inverse = lax.rsqrt(square)
    inverse = inverse * (1.5 - 0.5 * square * (inverse * inverse))
    half_up = 0.5 + 0.5 * jnp.abs(d) * inverse
    root = lax.rsqrt(half_up)
    large = half_up * root
    small = 0.5 * jnp.abs(y) * inverse * root
    unit = 1.5 - 0.5 * (large * large + small * small)
    large = large * unit
    small = small * unit
    ahead = d >= 0.0
    cosine = jnp.where(ahead, large, small)
    sine = jnp.where(ahead, small, large)
    return cosine, jnp.where((y < 0.0) == lower, -sine, sine)


def permuted(value, index):
    return jnp.take_along_axis(value, index, axis=1, mode="promise_in_bounds")


def sweep(gram, table_ref):
    shape = (WIDTH, LANES)
    row = lax.broadcasted_iota(jnp.int32, shape, 0)
    lane = lax.broadcasted_iota(jnp.int32, shape, 1)
    own_mask = row == lane
    any_own_mask = row == lane % WIDTH
    lane_row = lax.broadcasted_iota(jnp.int32, (1, LANES), 1)

    def at_mask(mask, value):
        return jnp.sum(jnp.where(mask, value, 0.0), axis=0, keepdims=True)

    def to_front(value, group):
        return pltpu.roll(value, LANES - WIDTH * group, 1)

    def step(k, state):
        gram, turning, own, other, cross = state
        table = table_ref[pl.ds(k, 1), :]
        partners = table_ref[pl.ds(k + WIDTH, 1), :]
        index = jnp.broadcast_to(table, shape)
        partner_mask = row == jnp.broadcast_to(partners, shape)
        crossed = permuted(gram, index)
        from_own = at_mask(any_own_mask, crossed)
        from_partner = at_mask(partner_mask, crossed)
        next_row = jnp.broadcast_to(to_front(table, 1), (8, LANES))

        def at_next(value):
            return permuted(jnp.broadcast_to(value, (8, LANES)), next_row)[:1]

        own_q, own_pq = to_front(from_own, 1), to_front(from_own, 2)
        partner_q, partner_pq = to_front(from_partner, 1), to_front(from_partner, 2)
        both_own = 0.5 * (own_q + at_next(own_q))
        both_partner = 0.5 * (partner_pq + at_next(partner_pq))
        ahead = 0.5 * (own_pq + at_next(partner_q))
        behind = 0.5 * (partner_q + at_next(own_pq))
        cosine, sine = turn_of(own, other, cross, lane_row < table)
        cosine_q, sine_q = at_next(cosine), at_next(sine)
        next_own = own + sine * (2.0 * cosine * cross - sine * (own - other))
        next_other = at_next(next_own)
        next_cross = (((cosine * cosine_q) * both_own + (sine * sine_q) * both_partner)
                      + ((cosine * sine_q) * ahead + (sine * cosine_q) * behind))
        half_done = gram * cosine + crossed * sine
        flipped = half_done.T[:WIDTH]
        flipped = jnp.concatenate([flipped, jnp.zeros((WIDTH, LANES - WIDTH), jnp.float32)], axis=1)
        gram = flipped * cosine + permuted(flipped, index) * sine
        turning = turning * cosine + permuted(turning, index) * sine
        return gram, turning, next_own, next_other, next_cross

    start = jnp.where(own_mask, 1.0, 0.0).astype(jnp.float32)
    first = jnp.broadcast_to(table_ref[pl.ds(0, 1), :], shape)
    crossed = permuted(gram, first)
    cross = at_mask(own_mask, crossed)
    cross = 0.5 * (cross + permuted(jnp.broadcast_to(cross, (8, LANES)), first[:8])[:1])
    state = (gram, start, at_mask(own_mask, gram), at_mask(row == first, crossed), cross)
    return lax.fori_loop(0, WIDTH - 1, step, state)[1]


def step_table(plan):
    same = jnp.arange(WIDTH, dtype=jnp.int32)
    following = jnp.concatenate([plan[1:], same[None]], axis=0)
    both = jnp.take_along_axis(plan, following, axis=1)
    still = jnp.broadcast_to(same, plan.shape)
    table = jnp.concatenate([plan, following, both, still], axis=1)
    blank = jnp.zeros((1, LANES), jnp.int32)
    return jnp.concatenate([table, blank, jnp.tile(plan, (1, LANES // WIDTH)), blank], axis=0)


def kernel(groups, blocks, snap_ref, plan_ref, out_ref, mode_ref,
           current, rotated, inner_slots, outer_slots,
           inner_send, inner_recv, outer_send, outer_recv, move_send, move_recv):
    cell = lax.axis_index("cell")
    pair = lax.axis_index("blk")
    inner = lax.rem(cell, INNER)
    outer = cell // INNER
    base = outer * INNER

    def inner_peer(offset):
        return lax.rem(inner + offset, INNER)

    def outer_peer(offset):
        return lax.rem(outer + offset, groups)

    barrier = pltpu.get_barrier_semaphore()
    for offset in range(1, INNER):
        pl.semaphore_signal(barrier, inc=1, device_id=(base + inner_peer(offset), pair), device_id_type=MESH)
    for offset in range(1, groups):
        pl.semaphore_signal(barrier, inc=1, device_id=(outer_peer(offset) * INNER + inner, pair), device_id_type=MESH)

    for step in (1, blocks - 1):
        pl.semaphore_signal(barrier, inc=1, device_id=(cell, lax.rem(pair + step, blocks)), device_id_type=MESH)
    pl.semaphore_wait(barrier, INNER - 1 + groups - 1 + 2)

    def inner_copy(slot, whose, peer, offset):
        return pltpu.make_async_remote_copy(
            src_ref=inner_slots.at[slot, whose], dst_ref=inner_slots.at[slot, whose],
            send_sem=inner_send.at[slot, offset], recv_sem=inner_recv.at[slot, whose],
            device_id=(base + peer, pair), device_id_type=MESH)

    def outer_copy(slot, whose, peer, offset):
        return pltpu.make_async_remote_copy(
            src_ref=outer_slots.at[slot, whose], dst_ref=outer_slots.at[slot, whose],
            send_sem=outer_send.at[slot, offset], recv_sem=outer_recv.at[slot, whose],
            device_id=(peer * INNER + inner, pair), device_id_type=MESH)

    def chunk_gram(slot, chunk):
        block = current[slot, chunk].reshape(WIDTH, -1)
        return lax.dot_general(block, block, (((1,), (1,)), ((), ())), precision=HIGHEST,
                               preferred_element_type=jnp.float32)

    def summed_gram(slot, gram):
        packed = jnp.concatenate([gram[8 * i:8 * i + 8] for i in range(4)], axis=1)
        inner_slots[slot, inner] = packed
        for offset in range(1, INNER):
            inner_copy(slot, inner, inner_peer(offset), offset).start()
        for offset in range(1, INNER):
            inner_copy(slot, inner_peer(offset), inner_peer(offset), offset).wait_recv()
        total = inner_slots[slot, 0]
        for i in range(1, INNER):
            total = total + inner_slots[slot, i]
        outer_slots[slot, outer] = total
        for offset in range(1, groups):
            outer_copy(slot, outer, outer_peer(offset), offset).start()
        for offset in range(1, groups):
            outer_copy(slot, outer_peer(offset), outer_peer(offset), offset).wait_recv()
        total = outer_slots[slot, 0]
        for i in range(1, groups):
            total = total + outer_slots[slot, i]
        for offset in range(1, INNER):
            inner_copy(slot, inner, inner_peer(offset), offset).wait_send()
        for offset in range(1, groups):
            outer_copy(slot, outer, outer_peer(offset), offset).wait_send()
        return jnp.concatenate(
            [total] + [pltpu.roll(total, LANES - WIDTH * i, 1) for i in range(1, 4)], axis=0)

    def right_copy(after, chunk):
        return pltpu.make_async_remote_copy(
            src_ref=rotated.at[chunk, jnp.where(pair == 0, 1, 0)], dst_ref=current.at[after, chunk, 0],
            send_sem=move_send.at[0, chunk], recv_sem=move_recv.at[after, 0, chunk],
            device_id=(cell, jnp.minimum(pair + 1, blocks - 1)), device_id_type=MESH)

    def left_copy(after, chunk):
        return pltpu.make_async_remote_copy(
            src_ref=rotated.at[chunk, 1], dst_ref=current.at[after, chunk, 1],
            send_sem=move_send.at[1, chunk], recv_sem=move_recv.at[after, 1, chunk],
            device_id=(cell, jnp.maximum(pair - 1, 0)), device_id_type=MESH)

    width = current.shape[-1]
    first_gram = jnp.zeros((WIDTH, WIDTH), jnp.float32)
    for chunk in range(CHUNKS):
        current[0, chunk] = snap_ref[:, chunk * width:(chunk + 1) * width].reshape(2, HALF, width)
        first_gram = first_gram + chunk_gram(0, chunk)

    def one_round(r, gram):
        now = lax.rem(r, 2)
        after = 1 - now
        turning = sweep(summed_gram(now, gram), plan_ref)[:, :WIDTH]
        for chunk in range(CHUNKS):
            block = current[now, chunk].reshape(WIDTH, width)
            turned = lax.dot_general(turning, block, (((0,), (0,)), ((), ())), precision=HIGHEST,
                                     preferred_element_type=jnp.float32)
            rotated[chunk] = turned.reshape(2, HALF, width)

            @pl.when(pair < blocks - 1)
            def _():
                right_copy(after, chunk).start()

            @pl.when(pair > 0)
            def _():
                left_copy(after, chunk).start()

        @pl.when(pair == 0)
        def _():
            for chunk in range(CHUNKS):
                current[after, chunk, 0] = rotated[chunk, 0]

        @pl.when(pair == blocks - 1)
        def _():
            for chunk in range(CHUNKS):
                current[after, chunk, 1] = rotated[chunk, 0]

        gram = jnp.zeros((WIDTH, WIDTH), jnp.float32)
        for chunk in range(CHUNKS):
            @pl.when(pair > 0)
            def _():
                right_copy(after, chunk).wait_recv()

            @pl.when(pair < blocks - 1)
            def _():
                left_copy(after, chunk).wait_recv()

            gram = gram + chunk_gram(after, chunk)

        for chunk in range(CHUNKS):
            @pl.when(pair > 0)
            def _():
                left_copy(after, chunk).wait_send()

            @pl.when(pair < blocks - 1)
            def _():
                right_copy(after, chunk).wait_send()

        return gram

    gram = lax.fori_loop(0, ROUNDS, one_round, first_gram)
    last = ROUNDS % 2
    gram = summed_gram(last, gram)
    row = lax.broadcasted_iota(jnp.int32, (WIDTH, LANES), 0)
    lane = lax.broadcasted_iota(jnp.int32, (WIDTH, LANES), 1)
    mode_ref[...] = jnp.sum(jnp.where(row == lane, gram, 0.0), axis=0, keepdims=True)
    for chunk in range(CHUNKS):
        out_ref[:, chunk * width:(chunk + 1) * width] = current[last, chunk].reshape(WIDTH, width)


def on_device(snapshots, plan):
    cells = lax.axis_size("cell")
    blocks = lax.axis_size("blk")
    groups = cells // INNER
    local = snapshots.shape[1]
    field, energy = pl.pallas_call(
        functools.partial(kernel, groups, blocks),
        out_shape=(jax.ShapeDtypeStruct((WIDTH, local), jnp.float32),
                   jax.ShapeDtypeStruct((1, LANES), jnp.float32)),
        in_specs=[pl.BlockSpec(memory_space=pltpu.VMEM)] * 2,
        out_specs=(pl.BlockSpec(memory_space=pltpu.VMEM),) * 2,
        scratch_shapes=[
            pltpu.VMEM((2, CHUNKS, 2, HALF, local // CHUNKS), jnp.float32),
            pltpu.VMEM((CHUNKS, 2, HALF, local // CHUNKS), jnp.float32),
            pltpu.VMEM((2, INNER, 8, LANES), jnp.float32),
            pltpu.VMEM((2, groups, 8, LANES), jnp.float32),
            pltpu.SemaphoreType.DMA((2, INNER)),
            pltpu.SemaphoreType.DMA((2, INNER)),
            pltpu.SemaphoreType.DMA((2, groups)),
            pltpu.SemaphoreType.DMA((2, groups)),
            pltpu.SemaphoreType.DMA((2, CHUNKS)),
            pltpu.SemaphoreType.DMA((2, 2, CHUNKS)),
        ],
        compiler_params=pltpu.CompilerParams(collective_id=0, has_side_effects=True),
        name="rounds",
    )(snapshots, step_table(plan))
    return field * field, energy[0, :WIDTH] / (local * cells)


def solution(mesh):
    return jax.shard_map(
        on_device,
        mesh=mesh,
        in_specs=(P("blk", "cell"), P()),
        out_specs=(P("blk", "cell"), P("blk")),
        check_vma=False,
    )
```

```python
import functools

import jax
import jax.numpy as jnp
from jax import lax
from jax.experimental import pallas as pl
from jax.experimental.pallas import tpu as pltpu
from jax.sharding import PartitionSpec as P

ROUNDS = 7
INNER = 2
WIDTH = 32
HALF = 16
LANES = 128
CHUNKS = 4
MESH = pl.DeviceIdType.MESH
HIGHEST = lax.Precision.HIGHEST


def turn_of(own, other, cross, lower):
    difference = own - other
    spread = jnp.where(lower, difference, -difference)
    height = 2.0 * cross
    size = jnp.maximum(jnp.abs(height), jnp.abs(spread))
    nothing = size == 0.0
    factor = pl.reciprocal(jnp.where(nothing, 1.0, size), approx=True)
    y = height * factor
    d = jnp.where(nothing, 1.0, spread * factor)
    square = y * y + d * d
    inverse = lax.rsqrt(square)
    inverse = inverse * (1.5 - 0.5 * square * (inverse * inverse))
    half_up = 0.5 + 0.5 * jnp.abs(d) * inverse
    root = lax.rsqrt(half_up)
    large = half_up * root
    small = 0.5 * jnp.abs(y) * inverse * root
    unit = 1.5 - 0.5 * (large * large + small * small)
    large = large * unit
    small = small * unit
    ahead = d >= 0.0
    cosine = jnp.where(ahead, large, small)
    sine = jnp.where(ahead, small, large)
    return cosine, jnp.where((y < 0.0) == lower, -sine, sine)


def permuted(value, index):
    return jnp.take_along_axis(value, index, axis=1, mode="promise_in_bounds")


def sweep(gram, table_ref):
    shape = (WIDTH, LANES)
    row = lax.broadcasted_iota(jnp.int32, shape, 0)
    lane = lax.broadcasted_iota(jnp.int32, shape, 1)
    own_mask = row == lane
    any_own_mask = row == lane % WIDTH
    lane_row = lax.broadcasted_iota(jnp.int32, (1, LANES), 1)

    def at_mask(mask, value):
        return jnp.sum(jnp.where(mask, value, 0.0), axis=0, keepdims=True)

    def to_front(value, group):
        return pltpu.roll(value, LANES - WIDTH * group, 1)

    upper_rows = lax.broadcasted_iota(jnp.int32, (8, LANES), 0) < 4

    def two_rows(first, second):
        return jnp.where(upper_rows, jnp.broadcast_to(first, (8, LANES)), jnp.broadcast_to(second, (8, LANES)))

    def step(k, state):
        gram, turning, own, other, cross = state
        table = table_ref[pl.ds(k, 1), :]
        partners = table_ref[pl.ds(k + WIDTH, 1), :]
        index = jnp.broadcast_to(table, shape)
        partner_mask = row == jnp.broadcast_to(partners, shape)
        crossed = permuted(gram, index)
        from_own = at_mask(any_own_mask, crossed)
        from_partner = at_mask(partner_mask, crossed)
        next_row = jnp.broadcast_to(table_ref[pl.ds(k + 2 * WIDTH, 1), :], (8, LANES))
        stack = two_rows(from_own, from_partner)
        at_q, at_pq = to_front(stack, 1), to_front(stack, 2)
        next_q, next_pq = permuted(stack, next_row + WIDTH), permuted(stack, next_row + 2 * WIDTH)
        own_q, partner_q = at_q[:1], at_q[4:5]
        own_pq, partner_pq = at_pq[:1], at_pq[4:5]
        both_own = 0.5 * (own_q + next_q[:1])
        both_partner = 0.5 * (partner_pq + next_pq[4:5])
        ahead = 0.5 * (own_pq + next_q[4:5])
        behind = 0.5 * (partner_q + next_pq[:1])
        cosine, sine = turn_of(own, other, cross, lane_row < table)
        next_turn = permuted(two_rows(cosine, sine), next_row)
        cosine_q, sine_q = next_turn[:1], next_turn[4:5]
        next_own = own + sine * (2.0 * cosine * cross - sine * (own - other))
        next_other = permuted(jnp.broadcast_to(next_own, (8, LANES)), next_row)[:1]
        next_cross = (((cosine * cosine_q) * both_own + (sine * sine_q) * both_partner)
                      + ((cosine * sine_q) * ahead + (sine * cosine_q) * behind))
        half_done = gram * cosine + crossed * sine
        flipped = half_done.T[:WIDTH]
        flipped = jnp.concatenate([flipped, jnp.zeros((WIDTH, LANES - WIDTH), jnp.float32)], axis=1)
        gram = flipped * cosine + permuted(flipped, index) * sine
        turning = turning * cosine + permuted(turning, index) * sine
        return gram, turning, next_own, next_other, next_cross

    start = jnp.where(own_mask, 1.0, 0.0).astype(jnp.float32)
    first = jnp.broadcast_to(table_ref[pl.ds(0, 1), :], shape)
    crossed = permuted(gram, first)
    cross = at_mask(own_mask, crossed)
    cross = 0.5 * (cross + permuted(jnp.broadcast_to(cross, (8, LANES)), first[:8])[:1])
    state = (gram, start, at_mask(own_mask, gram), at_mask(row == first, crossed), cross)
    return lax.fori_loop(0, WIDTH - 1, step, state)[1]


def step_table(plan):
    same = jnp.arange(WIDTH, dtype=jnp.int32)
    following = jnp.concatenate([plan[1:], same[None]], axis=0)
    both = jnp.take_along_axis(plan, following, axis=1)
    still = jnp.broadcast_to(same, plan.shape)
    table = jnp.concatenate([plan, following, both, still], axis=1)
    blank = jnp.zeros((1, LANES), jnp.int32)
    return jnp.concatenate([table, blank, jnp.tile(plan, (1, LANES // WIDTH)), blank,
                            jnp.tile(following, (1, LANES // WIDTH)), blank], axis=0)


def kernel(groups, blocks, snap_ref, plan_ref, out_ref, mode_ref,
           current, rotated, inner_slots, outer_slots,
           inner_send, inner_recv, outer_send, outer_recv, move_send, move_recv):
    cell = lax.axis_index("cell")
    pair = lax.axis_index("blk")
    inner = lax.rem(cell, INNER)
    outer = cell // INNER
    base = outer * INNER

    def inner_peer(offset):
        return lax.rem(inner + offset, INNER)

    def outer_peer(offset):
        return lax.rem(outer + offset, groups)

    barrier = pltpu.get_barrier_semaphore()
    for offset in range(1, INNER):
        pl.semaphore_signal(barrier, inc=1, device_id=(base + inner_peer(offset), pair), device_id_type=MESH)
    for offset in range(1, groups):
        pl.semaphore_signal(barrier, inc=1, device_id=(outer_peer(offset) * INNER + inner, pair), device_id_type=MESH)

    for step in (1, blocks - 1):
        pl.semaphore_signal(barrier, inc=1, device_id=(cell, lax.rem(pair + step, blocks)), device_id_type=MESH)
    pl.semaphore_wait(barrier, INNER - 1 + groups - 1 + 2)

    def inner_copy(slot, whose, peer, offset):
        return pltpu.make_async_remote_copy(
            src_ref=inner_slots.at[slot, whose], dst_ref=inner_slots.at[slot, whose],
            send_sem=inner_send.at[slot, offset], recv_sem=inner_recv.at[slot, whose],
            device_id=(base + peer, pair), device_id_type=MESH)

    def outer_copy(slot, whose, peer, offset):
        return pltpu.make_async_remote_copy(
            src_ref=outer_slots.at[slot, whose], dst_ref=outer_slots.at[slot, whose],
            send_sem=outer_send.at[slot, offset], recv_sem=outer_recv.at[slot, whose],
            device_id=(peer * INNER + inner, pair), device_id_type=MESH)

    def chunk_gram(slot, chunk):
        block = current[slot, chunk].reshape(WIDTH, -1)
        return lax.dot_general(block, block, (((1,), (1,)), ((), ())), precision=HIGHEST,
                               preferred_element_type=jnp.float32)

    def summed_gram(slot, gram):
        packed = jnp.concatenate([gram[8 * i:8 * i + 8] for i in range(4)], axis=1)
        inner_slots[slot, inner] = packed
        for offset in range(1, INNER):
            inner_copy(slot, inner, inner_peer(offset), offset).start()
        for offset in range(1, INNER):
            inner_copy(slot, inner_peer(offset), inner_peer(offset), offset).wait_recv()
        total = inner_slots[slot, 0]
        for i in range(1, INNER):
            total = total + inner_slots[slot, i]
        outer_slots[slot, outer] = total
        for offset in range(1, groups):
            outer_copy(slot, outer, outer_peer(offset), offset).start()
        for offset in range(1, groups):
            outer_copy(slot, outer_peer(offset), outer_peer(offset), offset).wait_recv()
        total = outer_slots[slot, 0]
        for i in range(1, groups):
            total = total + outer_slots[slot, i]
        for offset in range(1, INNER):
            inner_copy(slot, inner, inner_peer(offset), offset).wait_send()
        for offset in range(1, groups):
            outer_copy(slot, outer, outer_peer(offset), offset).wait_send()
        return jnp.concatenate(
            [total] + [pltpu.roll(total, LANES - WIDTH * i, 1) for i in range(1, 4)], axis=0)

    def right_copy(after, chunk):
        return pltpu.make_async_remote_copy(
            src_ref=rotated.at[chunk, jnp.where(pair == 0, 1, 0)], dst_ref=current.at[after, chunk, 0],
            send_sem=move_send.at[0, chunk], recv_sem=move_recv.at[after, 0, chunk],
            device_id=(cell, jnp.minimum(pair + 1, blocks - 1)), device_id_type=MESH)

    def left_copy(after, chunk):
        return pltpu.make_async_remote_copy(
            src_ref=rotated.at[chunk, 1], dst_ref=current.at[after, chunk, 1],
            send_sem=move_send.at[1, chunk], recv_sem=move_recv.at[after, 1, chunk],
            device_id=(cell, jnp.maximum(pair - 1, 0)), device_id_type=MESH)

    width = current.shape[-1]
    first_gram = jnp.zeros((WIDTH, WIDTH), jnp.float32)
    for chunk in range(CHUNKS):
        current[0, chunk] = snap_ref[:, chunk * width:(chunk + 1) * width].reshape(2, HALF, width)
        first_gram = first_gram + chunk_gram(0, chunk)

    def one_round(r, gram):
        now = lax.rem(r, 2)
        after = 1 - now
        turning = sweep(summed_gram(now, gram), plan_ref)[:, :WIDTH]
        for chunk in range(CHUNKS):
            block = current[now, chunk].reshape(WIDTH, width)
            turned = lax.dot_general(turning, block, (((0,), (0,)), ((), ())), precision=HIGHEST,
                                     preferred_element_type=jnp.float32)
            rotated[chunk] = turned.reshape(2, HALF, width)

            @pl.when(pair < blocks - 1)
            def _():
                right_copy(after, chunk).start()

            @pl.when(pair > 0)
            def _():
                left_copy(after, chunk).start()

        @pl.when(pair == 0)
        def _():
            for chunk in range(CHUNKS):
                current[after, chunk, 0] = rotated[chunk, 0]

        @pl.when(pair == blocks - 1)
        def _():
            for chunk in range(CHUNKS):
                current[after, chunk, 1] = rotated[chunk, 0]

        gram = jnp.zeros((WIDTH, WIDTH), jnp.float32)
        for chunk in range(CHUNKS):
            @pl.when(pair > 0)
            def _():
                right_copy(after, chunk).wait_recv()

            @pl.when(pair < blocks - 1)
            def _():
                left_copy(after, chunk).wait_recv()

            gram = gram + chunk_gram(after, chunk)

        for chunk in range(CHUNKS):
            @pl.when(pair > 0)
            def _():
                left_copy(after, chunk).wait_send()

            @pl.when(pair < blocks - 1)
            def _():
                right_copy(after, chunk).wait_send()

        return gram

    gram = lax.fori_loop(0, ROUNDS, one_round, first_gram)
    last = ROUNDS % 2
    gram = summed_gram(last, gram)
    row = lax.broadcasted_iota(jnp.int32, (WIDTH, LANES), 0)
    lane = lax.broadcasted_iota(jnp.int32, (WIDTH, LANES), 1)
    mode_ref[...] = jnp.sum(jnp.where(row == lane, gram, 0.0), axis=0, keepdims=True)
    for chunk in range(CHUNKS):
        out_ref[:, chunk * width:(chunk + 1) * width] = current[last, chunk].reshape(WIDTH, width)


def on_device(snapshots, plan):
    cells = lax.axis_size("cell")
    blocks = lax.axis_size("blk")
    groups = cells // INNER
    local = snapshots.shape[1]
    field, energy = pl.pallas_call(
        functools.partial(kernel, groups, blocks),
        out_shape=(jax.ShapeDtypeStruct((WIDTH, local), jnp.float32),
                   jax.ShapeDtypeStruct((1, LANES), jnp.float32)),
        in_specs=[pl.BlockSpec(memory_space=pltpu.VMEM)] * 2,
        out_specs=(pl.BlockSpec(memory_space=pltpu.VMEM),) * 2,
        scratch_shapes=[
            pltpu.VMEM((2, CHUNKS, 2, HALF, local // CHUNKS), jnp.float32),
            pltpu.VMEM((CHUNKS, 2, HALF, local // CHUNKS), jnp.float32),
            pltpu.VMEM((2, INNER, 8, LANES), jnp.float32),
            pltpu.VMEM((2, groups, 8, LANES), jnp.float32),
            pltpu.SemaphoreType.DMA((2, INNER)),
            pltpu.SemaphoreType.DMA((2, INNER)),
            pltpu.SemaphoreType.DMA((2, groups)),
            pltpu.SemaphoreType.DMA((2, groups)),
            pltpu.SemaphoreType.DMA((2, CHUNKS)),
            pltpu.SemaphoreType.DMA((2, 2, CHUNKS)),
        ],
        compiler_params=pltpu.CompilerParams(collective_id=0, has_side_effects=True),
        name="rounds",
    )(snapshots, step_table(plan))
    return field * field, energy[0, :WIDTH] / (local * cells)


def solution(mesh):
    return jax.shard_map(
        on_device,
        mesh=mesh,
        in_specs=(P("blk", "cell"), P()),
        out_specs=(P("blk", "cell"), P("blk")),
        check_vma=False,
    )
```

```python
import functools

import jax
import jax.numpy as jnp
from jax import lax
from jax.experimental import pallas as pl
from jax.experimental.pallas import tpu as pltpu
from jax.sharding import PartitionSpec as P

ROUNDS = 7
INNER = 2
WIDTH = 32
HALF = 16
LANES = 128
CHUNKS = 2
MESH = pl.DeviceIdType.MESH
HIGHEST = lax.Precision.HIGHEST


def turn_of(own, other, cross, lower):
    difference = own - other
    spread = jnp.where(lower, difference, -difference)
    height = 2.0 * cross
    size = jnp.maximum(jnp.abs(height), jnp.abs(spread))
    nothing = size == 0.0
    factor = pl.reciprocal(jnp.where(nothing, 1.0, size), approx=True)
    y = height * factor
    d = jnp.where(nothing, 1.0, spread * factor)
    square = y * y + d * d
    inverse = lax.rsqrt(square)
    inverse = inverse * (1.5 - 0.5 * square * (inverse * inverse))
    half_up = 0.5 + 0.5 * jnp.abs(d) * inverse
    root = lax.rsqrt(half_up)
    large = half_up * root
    small = 0.5 * jnp.abs(y) * inverse * root
    unit = 1.5 - 0.5 * (large * large + small * small)
    large = large * unit
    small = small * unit
    ahead = d >= 0.0
    cosine = jnp.where(ahead, large, small)
    sine = jnp.where(ahead, small, large)
    return cosine, jnp.where((y < 0.0) == lower, -sine, sine)


def permuted(value, index):
    return jnp.take_along_axis(value, index, axis=1, mode="promise_in_bounds")


def sweep(gram, table_ref):
    shape = (WIDTH, LANES)
    row = lax.broadcasted_iota(jnp.int32, shape, 0)
    lane = lax.broadcasted_iota(jnp.int32, shape, 1)
    own_mask = row == lane
    any_own_mask = row == lane % WIDTH
    lane_row = lax.broadcasted_iota(jnp.int32, (1, LANES), 1)

    def at_mask(mask, value):
        return jnp.sum(jnp.where(mask, value, 0.0), axis=0, keepdims=True)

    def to_front(value, group):
        return pltpu.roll(value, LANES - WIDTH * group, 1)

    upper_rows = lax.broadcasted_iota(jnp.int32, (8, LANES), 0) < 4

    def two_rows(first, second):
        return jnp.where(upper_rows, jnp.broadcast_to(first, (8, LANES)), jnp.broadcast_to(second, (8, LANES)))

    def step(k, state):
        gram, turning, own, other, cross = state
        table = table_ref[pl.ds(k, 1), :]
        partners = table_ref[pl.ds(k + WIDTH, 1), :]
        index = jnp.broadcast_to(table, shape)
        partner_mask = row == jnp.broadcast_to(partners, shape)
        crossed = permuted(gram, index)
        from_own = at_mask(any_own_mask, crossed)
        from_partner = at_mask(partner_mask, crossed)
        next_row = jnp.broadcast_to(table_ref[pl.ds(k + 2 * WIDTH, 1), :], (8, LANES))
        stack = two_rows(from_own, from_partner)
        at_q, at_pq = to_front(stack, 1), to_front(stack, 2)
        next_q, next_pq = permuted(stack, next_row + WIDTH), permuted(stack, next_row + 2 * WIDTH)
        own_q, partner_q = at_q[:1], at_q[4:5]
        own_pq, partner_pq = at_pq[:1], at_pq[4:5]
        both_own = 0.5 * (own_q + next_q[:1])
        both_partner = 0.5 * (partner_pq + next_pq[4:5])
        ahead = 0.5 * (own_pq + next_q[4:5])
        behind = 0.5 * (partner_q + next_pq[:1])
        cosine, sine = turn_of(own, other, cross, lane_row < table)
        next_turn = permuted(two_rows(cosine, sine), next_row)
        cosine_q, sine_q = next_turn[:1], next_turn[4:5]
        next_own = own + sine * (2.0 * cosine * cross - sine * (own - other))
        next_other = permuted(jnp.broadcast_to(next_own, (8, LANES)), next_row)[:1]
        next_cross = (((cosine * cosine_q) * both_own + (sine * sine_q) * both_partner)
                      + ((cosine * sine_q) * ahead + (sine * cosine_q) * behind))
        half_done = gram * cosine + crossed * sine
        flipped = half_done.T[:WIDTH]
        flipped = jnp.concatenate([flipped, jnp.zeros((WIDTH, LANES - WIDTH), jnp.float32)], axis=1)
        gram = flipped * cosine + permuted(flipped, index) * sine
        turning = turning * cosine + permuted(turning, index) * sine
        return gram, turning, next_own, next_other, next_cross

    start = jnp.where(own_mask, 1.0, 0.0).astype(jnp.float32)
    first = jnp.broadcast_to(table_ref[pl.ds(0, 1), :], shape)
    crossed = permuted(gram, first)
    cross = at_mask(own_mask, crossed)
    cross = 0.5 * (cross + permuted(jnp.broadcast_to(cross, (8, LANES)), first[:8])[:1])
    state = (gram, start, at_mask(own_mask, gram), at_mask(row == first, crossed), cross)
    return lax.fori_loop(0, WIDTH - 1, step, state)[1]


def step_table(plan):
    same = jnp.arange(WIDTH, dtype=jnp.int32)
    following = jnp.concatenate([plan[1:], same[None]], axis=0)
    both = jnp.take_along_axis(plan, following, axis=1)
    still = jnp.broadcast_to(same, plan.shape)
    table = jnp.concatenate([plan, following, both, still], axis=1)
    blank = jnp.zeros((1, LANES), jnp.int32)
    return jnp.concatenate([table, blank, jnp.tile(plan, (1, LANES // WIDTH)), blank,
                            jnp.tile(following, (1, LANES // WIDTH)), blank], axis=0)


def kernel(groups, blocks, snap_ref, plan_ref, out_ref, mode_ref,
           current, rotated, inner_slots, outer_slots,
           inner_send, inner_recv, outer_send, outer_recv, move_send, move_recv):
    cell = lax.axis_index("cell")
    pair = lax.axis_index("blk")
    inner = lax.rem(cell, INNER)
    outer = cell // INNER
    base = outer * INNER

    def inner_peer(offset):
        return lax.rem(inner + offset, INNER)

    def outer_peer(offset):
        return lax.rem(outer + offset, groups)

    barrier = pltpu.get_barrier_semaphore()
    for offset in range(1, INNER):
        pl.semaphore_signal(barrier, inc=1, device_id=(base + inner_peer(offset), pair), device_id_type=MESH)
    for offset in range(1, groups):
        pl.semaphore_signal(barrier, inc=1, device_id=(outer_peer(offset) * INNER + inner, pair), device_id_type=MESH)

    for step in (1, blocks - 1):
        pl.semaphore_signal(barrier, inc=1, device_id=(cell, lax.rem(pair + step, blocks)), device_id_type=MESH)
    pl.semaphore_wait(barrier, INNER - 1 + groups - 1 + 2)

    def inner_copy(slot, whose, peer, offset):
        return pltpu.make_async_remote_copy(
            src_ref=inner_slots.at[slot, whose], dst_ref=inner_slots.at[slot, whose],
            send_sem=inner_send.at[slot, offset], recv_sem=inner_recv.at[slot, whose],
            device_id=(base + peer, pair), device_id_type=MESH)

    def outer_copy(slot, whose, peer, offset):
        return pltpu.make_async_remote_copy(
            src_ref=outer_slots.at[slot, whose], dst_ref=outer_slots.at[slot, whose],
            send_sem=outer_send.at[slot, offset], recv_sem=outer_recv.at[slot, whose],
            device_id=(peer * INNER + inner, pair), device_id_type=MESH)

    def chunk_gram(slot, chunk):
        block = current[slot, chunk].reshape(WIDTH, -1)
        return lax.dot_general(block, block, (((1,), (1,)), ((), ())), precision=HIGHEST,
                               preferred_element_type=jnp.float32)

    def summed_gram(slot, gram):
        packed = jnp.concatenate([gram[8 * i:8 * i + 8] for i in range(4)], axis=1)
        inner_slots[slot, inner] = packed
        for offset in range(1, INNER):
            inner_copy(slot, inner, inner_peer(offset), offset).start()
        for offset in range(1, INNER):
            inner_copy(slot, inner_peer(offset), inner_peer(offset), offset).wait_recv()
        total = inner_slots[slot, 0]
        for i in range(1, INNER):
            total = total + inner_slots[slot, i]
        outer_slots[slot, outer] = total
        for offset in range(1, groups):
            outer_copy(slot, outer, outer_peer(offset), offset).start()
        for offset in range(1, groups):
            outer_copy(slot, outer_peer(offset), outer_peer(offset), offset).wait_recv()
        total = outer_slots[slot, 0]
        for i in range(1, groups):
            total = total + outer_slots[slot, i]
        for offset in range(1, INNER):
            inner_copy(slot, inner, inner_peer(offset), offset).wait_send()
        for offset in range(1, groups):
            outer_copy(slot, outer, outer_peer(offset), offset).wait_send()
        return jnp.concatenate(
            [total] + [pltpu.roll(total, LANES - WIDTH * i, 1) for i in range(1, 4)], axis=0)

    def right_copy(after, chunk):
        return pltpu.make_async_remote_copy(
            src_ref=rotated.at[chunk, jnp.where(pair == 0, 1, 0)], dst_ref=current.at[after, chunk, 0],
            send_sem=move_send.at[0, chunk], recv_sem=move_recv.at[after, 0, chunk],
            device_id=(cell, jnp.minimum(pair + 1, blocks - 1)), device_id_type=MESH)

    def left_copy(after, chunk):
        return pltpu.make_async_remote_copy(
            src_ref=rotated.at[chunk, 1], dst_ref=current.at[after, chunk, 1],
            send_sem=move_send.at[1, chunk], recv_sem=move_recv.at[after, 1, chunk],
            device_id=(cell, jnp.maximum(pair - 1, 0)), device_id_type=MESH)

    width = current.shape[-1]
    first_gram = jnp.zeros((WIDTH, WIDTH), jnp.float32)
    for chunk in range(CHUNKS):
        current[0, chunk] = snap_ref[:, chunk * width:(chunk + 1) * width].reshape(2, HALF, width)
        first_gram = first_gram + chunk_gram(0, chunk)

    def one_round(r, gram):
        now = lax.rem(r, 2)
        after = 1 - now
        turning = sweep(summed_gram(now, gram), plan_ref)[:, :WIDTH]
        for chunk in range(CHUNKS):
            block = current[now, chunk].reshape(WIDTH, width)
            turned = lax.dot_general(turning, block, (((0,), (0,)), ((), ())), precision=HIGHEST,
                                     preferred_element_type=jnp.float32)
            rotated[chunk] = turned.reshape(2, HALF, width)

            @pl.when(pair < blocks - 1)
            def _():
                right_copy(after, chunk).start()

            @pl.when(pair > 0)
            def _():
                left_copy(after, chunk).start()

        @pl.when(pair == 0)
        def _():
            for chunk in range(CHUNKS):
                current[after, chunk, 0] = rotated[chunk, 0]

        @pl.when(pair == blocks - 1)
        def _():
            for chunk in range(CHUNKS):
                current[after, chunk, 1] = rotated[chunk, 0]

        gram = jnp.zeros((WIDTH, WIDTH), jnp.float32)
        for chunk in range(CHUNKS):
            @pl.when(pair > 0)
            def _():
                right_copy(after, chunk).wait_recv()

            @pl.when(pair < blocks - 1)
            def _():
                left_copy(after, chunk).wait_recv()

            gram = gram + chunk_gram(after, chunk)

        for chunk in range(CHUNKS):
            @pl.when(pair > 0)
            def _():
                left_copy(after, chunk).wait_send()

            @pl.when(pair < blocks - 1)
            def _():
                right_copy(after, chunk).wait_send()

        return gram

    gram = lax.fori_loop(0, ROUNDS, one_round, first_gram)
    last = ROUNDS % 2
    gram = summed_gram(last, gram)
    row = lax.broadcasted_iota(jnp.int32, (WIDTH, LANES), 0)
    lane = lax.broadcasted_iota(jnp.int32, (WIDTH, LANES), 1)
    mode_ref[...] = jnp.sum(jnp.where(row == lane, gram, 0.0), axis=0, keepdims=True)
    for chunk in range(CHUNKS):
        out_ref[:, chunk * width:(chunk + 1) * width] = current[last, chunk].reshape(WIDTH, width)


def on_device(snapshots, plan):
    cells = lax.axis_size("cell")
    blocks = lax.axis_size("blk")
    groups = cells // INNER
    local = snapshots.shape[1]
    field, energy = pl.pallas_call(
        functools.partial(kernel, groups, blocks),
        out_shape=(jax.ShapeDtypeStruct((WIDTH, local), jnp.float32),
                   jax.ShapeDtypeStruct((1, LANES), jnp.float32)),
        in_specs=[pl.BlockSpec(memory_space=pltpu.VMEM)] * 2,
        out_specs=(pl.BlockSpec(memory_space=pltpu.VMEM),) * 2,
        scratch_shapes=[
            pltpu.VMEM((2, CHUNKS, 2, HALF, local // CHUNKS), jnp.float32),
            pltpu.VMEM((CHUNKS, 2, HALF, local // CHUNKS), jnp.float32),
            pltpu.VMEM((2, INNER, 8, LANES), jnp.float32),
            pltpu.VMEM((2, groups, 8, LANES), jnp.float32),
            pltpu.SemaphoreType.DMA((2, INNER)),
            pltpu.SemaphoreType.DMA((2, INNER)),
            pltpu.SemaphoreType.DMA((2, groups)),
            pltpu.SemaphoreType.DMA((2, groups)),
            pltpu.SemaphoreType.DMA((2, CHUNKS)),
            pltpu.SemaphoreType.DMA((2, 2, CHUNKS)),
        ],
        compiler_params=pltpu.CompilerParams(collective_id=0, has_side_effects=True),
        name="rounds",
    )(snapshots, step_table(plan))
    return field * field, energy[0, :WIDTH] / (local * cells)


def solution(mesh):
    return jax.shard_map(
        on_device,
        mesh=mesh,
        in_specs=(P("blk", "cell"), P()),
        out_specs=(P("blk", "cell"), P("blk")),
        check_vma=False,
    )
```
